256 devices in a mesh: tm: 128 (over y, x, z), rhs: 2 (over core).
Axes of the slice: x: 4, y: 4, z: 8, core: 2. Of those that a mesh axis runs over, the one named last changes fastest.
Arguments:
- diag_blocks: float32 [512, 384, 384], P('tm')
- couplings: float32 [512, 384, 384], P('tm'), as said below
- arrow_coupling: float32 [512, 256, 384], P('tm', 'rhs')
- right_sides: float32 [512, 384, 128], P('tm', None, 'rhs')
- arrow_block: float32 [256, 256], P('rhs'), may hold values from -6 to 6
- arrow_rhs: float32 [256, 128], P(None, 'rhs'), may hold values from -6 to 6
Outputs:
- block_results: float32 [512, 384, 384], P('tm')
- coupling_results: float32 [512, 384, 384], P('tm')
- arrow_results: float32 [512, 256, 384], P('tm', 'rhs')
- rhs_results: float32 [512, 384, 128], P('tm', None, 'rhs')
- reduced_arrow: float32 [256, 256], P('rhs')
- reduced_arrow_rhs: float32 [256, 128], P(None, 'rhs')
The draws below stay inside these ranges and needn't reach their ends.
Inputs may be any that keep to these rules, and one draw needn't show every extreme that they name: couplings[0] is zero.
All inputs are finite; a program needn't handle non-finite values. Where the reference program divides by a largest or mean magnitude, that divisor is 1e-20 or more.
Results may differ from the reference program's by a relative error of at most 0.0001.
Values sent between devices are 32-bit elements; how exact they have to be, the bound alone decides.
No kernel may reach another device: no remote copies, remote signals or barrier semaphores. Data moves between devices by JAX's collectives and lax.ppermute only.
A program may use at most 64 MiB of HBM per device.

```python
import jax
import jax.numpy as jnp
from jax import lax

B = 384
A = 256
R = 128
ITERS = 12
LEVELS = 2
T_SIZE = 512


def scale_roots(key):
    logs = jax.random.uniform(jax.random.fold_in(key, 101), (T_SIZE, B), jnp.float32, jnp.log(0.05), jnp.log(20.0))
    return jnp.sqrt(jnp.exp(logs))


def draw_diag_blocks(key, part):
    roots = scale_roots(key)
    noise = jax.random.uniform(jax.random.fold_in(key, 11), (T_SIZE, B, B), jnp.float32, -1.0, 1.0)
    inner = (noise + 0.6 * jnp.swapaxes(noise, 1, 2)) * (0.8 / B ** 0.5) + 2.5 * jnp.eye(B, dtype=jnp.float32)[None]
    return inner * roots[:, :, None] * roots[:, None, :]


def draw_couplings(key, part):
    roots = scale_roots(key)
    earlier = jnp.concatenate([roots[:1], roots[:-1]], axis=0)
    inner = jax.random.uniform(jax.random.fold_in(key, 22), (T_SIZE, B, B), jnp.float32, -1.0, 1.0) * (0.45 / B ** 0.5)
    keep_mask = (jnp.arange(T_SIZE) > 0).astype(jnp.float32)
    return inner * roots[:, :, None] * earlier[:, None, :] * keep_mask[:, None, None]


def draw_arrow_coupling(key, part):
    roots = scale_roots(key)
    ramp = jnp.sqrt(1.0 + 2.0 * jnp.arange(T_SIZE).astype(jnp.float32) / (T_SIZE - 1))
    spread = ramp * jnp.sqrt(6.0 / (B * T_SIZE))
    noise = jax.random.uniform(jax.random.fold_in(key, 31), (T_SIZE, A, B), jnp.float32, -1.0, 1.0)
    return noise * spread[:, None, None] * roots[:, None, :]


def draw_right_sides(key, part):
    roots = scale_roots(key)
    noise = jax.random.normal(jax.random.fold_in(key, 41), (T_SIZE, B, R), jnp.float32)
    return noise * roots[:, :, None]


def levels(key, extent, cuts, low, high):
    loudness, own = 1.0, jax.random.fold_in(key, 6)
    for position, shards_of in cuts:
        steps = jnp.exp(jax.random.uniform(jax.random.fold_in(own, position), (shards_of,), jnp.float32, low / len(cuts), high / len(cuts)))
        loudness = loudness * jnp.repeat(steps, extent[position] // shards_of).reshape([-1 if axis == position else 1 for axis in range(len(extent))])
    return loudness


def scatter_about(own_key, dims, scale, bound, split=(), held_as=jnp.bfloat16):
    array = jax.random.normal(own_key, dims, jnp.float32) * scale
    if len(split) > 0:
        array = levels(own_key, dims, split, -0.22, 0.18) * array
    return jnp.clip(array, min=-bound, max=bound).astype(held_as)


def setup_inputs(seed: int = 0) -> dict:
    splits = jax.random.split(jax.random.key(seed), 7)
    return {
        "diag_blocks": draw_diag_blocks(jax.random.fold_in(splits[6], 71), 0),
        "couplings": draw_couplings(jax.random.fold_in(splits[6], 71), 0),
        "arrow_coupling": draw_arrow_coupling(jax.random.fold_in(splits[6], 71), 0),
        "right_sides": draw_right_sides(jax.random.fold_in(splits[6], 71), 0),
        "arrow_block": scatter_about(splits[4], (A, A), 1.0, 6.0, ((0, 2),), jnp.float32),
        "arrow_rhs": scatter_about(splits[5], (A, R), 1.0, 6.0, ((1, 2),), jnp.float32),
    }


def product(left, right):
    return jnp.matmul(left, right, precision=lax.Precision.HIGHEST)


def flipped(matrix):
    return jnp.swapaxes(matrix, -1, -2)


def newton_inverse(blocks):
    identity = jnp.eye(blocks.shape[-1], dtype=blocks.dtype)
    row_bound = jnp.max(jnp.sum(jnp.abs(blocks), axis=-1), axis=-1)
    start_guess = identity[None] / row_bound[:, None, None]

    def sweep(counter, approx):
        return 2.0 * approx - product(approx, product(blocks, approx))

    return lax.fori_loop(0, ITERS, sweep, start_guess)


def shifted_down(values):
    return jnp.concatenate([jnp.zeros_like(values[:1]), values[:-1]], axis=0)


def reduce_level(diagonal, coupling, arrow, right):
    inverse = newton_inverse(diagonal[1::2])
    own_coupling = coupling[1::2]
    next_coupling = jnp.concatenate([coupling[2::2], jnp.zeros_like(coupling[:1])], axis=0)
    multiplier = product(inverse, own_coupling)
    solved = product(inverse, right[1::2])
    weighted = product(arrow[1::2], inverse)
    left_diag = product(flipped(own_coupling), multiplier)
    left_right = product(flipped(own_coupling), solved)
    left_arrow = product(weighted, own_coupling)
    next_diag = product(product(next_coupling, inverse), flipped(next_coupling))
    next_link = -product(next_coupling, multiplier)
    next_arrow = product(weighted, flipped(next_coupling))
    next_right = product(next_coupling, solved)
    kept_state = (diagonal[0::2] - shifted_down(next_diag) - left_diag,
                  shifted_down(next_link),
                  arrow[0::2] - shifted_down(next_arrow) - left_arrow,
                  right[0::2] - shifted_down(next_right) - left_right)
    gone = (inverse, multiplier, weighted, solved)
    block_term = jnp.sum(product(weighted, flipped(arrow[1::2])), axis=0)
    right_term = jnp.sum(product(weighted, right[1::2]), axis=0)
    return kept_state, gone, block_term, right_term


def reference(diag_blocks, couplings, arrow_coupling, right_sides, arrow_block, arrow_rhs):
    state = (diag_blocks, couplings, arrow_coupling, right_sides)
    results = [jnp.zeros_like(whole) for whole in state]
    block_total = jnp.zeros_like(arrow_block)
    right_total = jnp.zeros_like(arrow_rhs)
    for level_no in range(LEVELS):
        stride = 2 ** level_no
        state, gone, block_term, right_term = reduce_level(state[0], state[1], state[2], state[3])
        results = [whole.at[stride::2 * stride].set(piece) for whole, piece in zip(results, gone)]
        block_total = block_total + block_term
        right_total = right_total + right_term
    final_stride = 2 ** LEVELS
    results = [whole.at[0::final_stride].set(piece) for whole, piece in zip(results, state)]
    return (results[0], results[1], results[2], results[3], arrow_block - block_total, arrow_rhs - right_total)
```

```python
import jax
import jax.numpy as jnp
from jax import lax
from jax.experimental import pallas as pl
from jax.experimental.pallas import tpu as pltpu
from jax.sharding import PartitionSpec as P


ITERS = 12
N = 384
HALF = 192
ROWS = 128
COLS = 64
F32 = jnp.float32
B16 = jnp.bfloat16
VMEM = 67043328
ROOM = 600 << 10


def dot(a, b, nt):
    dims = (((1,), (1 if nt else 0,)), ((), ()))
    return lax.dot_general(a, b, dims, preferred_element_type=F32)


def parts(x):
    high = x.astype(B16)
    return high, (x - high.astype(F32)).astype(B16)


def mm(a, b, nt=False):
    ah, al = parts(a)
    bh, bl = parts(b)
    n = b.shape[0] if nt else b.shape[1]
    if n % 128 == 0:
        both = dot(ah, jnp.concatenate([bh, bl], 0 if nt else 1), nt)
        return both[:, :n] + (both[:, n:] + dot(al, bh, nt))
    return dot(ah, bh, nt) + (dot(ah, bl, nt) + dot(al, bh, nt))


def newton(m_ref, x_ref):
    m = m_ref[...]
    row_bound = jnp.max(jnp.sum(jnp.abs(m), axis=1, keepdims=True), axis=0, keepdims=True)
    scale = 1.0 / row_bound
    eye = (
        lax.broadcasted_iota(jnp.int32, (N, N), 0) == lax.broadcasted_iota(jnp.int32, (N, N), 1)
    ).astype(F32)
    x_ref[...] = 2.0 * (eye * scale) - (m * scale) * scale

    def sweep(counter, carry):
        x = x_ref[...]
        residual = eye - mm(m_ref[...], x)
        x_ref[...] = x + mm(x, residual)
        return carry

    lax.fori_loop(0, ITERS - 1, sweep, 0)


class Feed:
    def __init__(self, core, sources, buf, sem):
        self.copy = pltpu.make_async_copy(sources[0], buf, sem)
        self.buf = buf
        self.ready = False
        if len(sources) == 1:
            self.copy.start()
        else:
            for which, source in enumerate(sources):

                @pl.when(core == which)
                def _(source=source):
                    pltpu.make_async_copy(source, buf, sem).start()

    def ref(self):
        if not self.ready:
            self.copy.wait()
            self.ready = True
        return self.buf

    def get(self):
        return self.ref()[...]


class Drain:
    def __init__(self, sems):
        self.sems = sems
        self.copies = []

    def send(self, src, dst):
        copy = pltpu.make_async_copy(src, dst, self.sems.at[len(self.copies)])
        copy.start()
        self.copies.append(copy)

    def finish(self):
        for copy in self.copies:
            copy.wait()


OUT_COPIES = 16


def call(body, me, ins, outs, scratch=(), units=1.0, alias=None, room=0):
    arrays = []
    places = []
    for shape, sources in ins:
        found = []
        for array, view in sources:
            for number, known in enumerate(arrays):
                if known is array:
                    break
            else:
                number = len(arrays)
                arrays.append(array)
            found.append((number, view))
        places.append(found)
    count = len(arrays)
    extra = list(alias or ())

    def kernel(core_ref, *refs):
        core = core_ref[0]
        given = refs[:count]
        outputs = refs[count + len(extra) : count + len(extra) + len(outs)]
        rest = refs[count + len(extra) + len(outs) :]
        bufs, held, in_sems, out_sems = rest[: len(ins)], rest[len(ins) : -2], rest[-2], rest[-1]
        feeds = [
            Feed(core, [view(given[number], core) for number, view in found], buf, in_sems.at[i])
            for i, (found, buf) in enumerate(zip(places, bufs))
        ]
        drain = Drain(out_sems)
        body(core, feeds, outputs, held, drain)
        drain.finish()

    moved = sum(4 * a.size for a in arrays)
    far = pl.BlockSpec(memory_space=pltpu.HBM)
    return pl.pallas_call(
        kernel,
        out_shape=[jax.ShapeDtypeStruct(shape, F32) for shape in outs],
        in_specs=[pl.BlockSpec(memory_space=pltpu.SMEM)] + [far] * (count + len(extra)),
        out_specs=[far] * len(outs),
        scratch_shapes=[pltpu.VMEM(shape, F32) for shape, sources in ins]
        + [pltpu.VMEM(shape, F32) for shape in scratch]
        + [pltpu.SemaphoreType.DMA((len(ins),)), pltpu.SemaphoreType.DMA((OUT_COPIES,))],
        input_output_aliases={1 + count + i: i for i in range(len(extra))},
        compiler_params=pltpu.CompilerParams(vmem_limit_bytes=VMEM - room),
        cost_estimate=pl.CostEstimate(flops=int(units * 6 * N**3), bytes_accessed=moved, transcendentals=0),
    )(me, *arrays, *extra)


def whole(ref, core):
    return ref


def rows(start, size):
    return lambda ref, core: ref.at[pl.ds(start, size)]


def at(index):
    return lambda ref, core: ref.at[index]


def own(ref, core):
    return ref.at[1 + 2 * core]


def core_rows(core, size):
    mine = pl.multiple_of(core * size, size)
    other = pl.multiple_of((1 - core) * size, size)
    return pl.ds(mine, size), pl.ds(other, size)


def inverse_body(core, ins, outs, held, drain):
    d, l, l0 = ins
    x_out, t_out, w_out, l0_out = outs
    x_s, t_s, w_s = held
    drain.send(l0.ref(), l0_out)
    newton(d.ref(), x_s)
    drain.send(x_s, x_out)
    l_ref = l.ref()

    @pl.when(core == 0)
    def _():
        w_s[...] = l_ref[...]

    @pl.when(core == 1)
    def _():
        w_s[...] = l_ref[...].T

    drain.send(w_s, w_out)
    w = w_s[...]
    t_s[...] = mm(mm(w, x_s[...]), w, nt=True)
    drain.send(t_s, t_out)


def own_body(core, ins, outs, held, drain):
    x_in, c_in, cx_in, b_in, bx_in, l_in, w_in = ins
    snd, keep = outs
    full, b_s, vz_s, gh_s, blk_s, y_s = held
    mine, other = core_rows(core, ROWS)
    full[mine, :] = c_in.get()
    full[other, :] = cx_in.get()
    b_s[0:COLS, :] = b_in.get()
    b_s[COLS:, :] = bx_in.get()
    x = x_in.get()
    drain.send(x_in.ref(), snd.at[pl.ds(0, N)])
    c = full[...]
    vz_s[0:256, :] = mm(c, x)
    vz_s[256:384, :] = mm(b_s[...], x, nt=True)
    drain.send(vz_s.at[other], snd.at[pl.ds(1024, ROWS)])
    drain.send(vz_s.at[pl.ds(320, COLS)], snd.at[pl.ds(1152, COLS)])
    drain.send(vz_s.at[mine], keep.at[pl.ds(0, ROWS)])
    drain.send(vz_s.at[pl.ds(256, COLS)], keep.at[pl.ds(128, COLS)])
    y_s[...] = mm(x, l_in.get())
    drain.send(y_s, snd.at[pl.ds(N, N)])
    vz = vz_s[...]
    gh_s[...] = mm(vz, w_in.get(), nt=True)
    drain.send(gh_s.at[pl.ds(0, 256)], snd.at[pl.ds(768, 256)])
    drain.send(gh_s.at[pl.ds(320, COLS)], snd.at[pl.ds(1216, COLS)])
    drain.send(gh_s.at[pl.ds(256, COLS)], keep.at[pl.ds(192, COLS)])
    blk_s[:, 0:256] = mm(vz, c, nt=True)
    drain.send(blk_s.at[other], snd.at[pl.ds(1280, ROWS)])
    drain.send(blk_s.at[pl.ds(320, COLS)], snd.at[pl.ds(1408, COLS)])
    drain.send(blk_s.at[mine], keep.at[pl.ds(256, ROWS)])
    drain.send(blk_s.at[pl.ds(256, COLS)], keep.at[pl.ds(384, COLS)])


def inverse2_body(core, ins, outs, held, drain):
    d, t, tx = ins
    m_s, x_s = held
    m_s[...] = d.get() - (t.get() + tx.get())
    newton(m_s, x_s)
    drain.send(x_s, outs[0])


def arrow_body(core, ins, outs, held, drain):
    x_in, c_in, cx_in, g, gx, b_in, hk, hr, bk, br, rk, rr = ins
    full, vz_s, s_s = held
    mine, other = core_rows(core, ROWS)
    full[mine, :] = c_in.get()
    full[other, :] = cx_in.get()
    full[...] = full[...] - (g.get() + gx.get())
    b = b_in.get() - (hk.get() + hr.get())
    x = x_in.get()
    vz_s[0:ROWS, :] = mm(full[mine, :], x)
    vz_s[ROWS:, :] = mm(b, x, nt=True)
    drain.send(vz_s, outs[0])
    sums = mm(vz_s[...], full[...], nt=True)
    s_s[0:ROWS, :] = sums[0:ROWS] + (bk.ref()[:, 0:256] + br.ref()[:, 0:256])
    s_s[ROWS:, :] = sums[ROWS:] + (rk.ref()[:, 0:256] + rr.ref()[:, 0:256])
    drain.send(s_s, outs[1])


def link_body(core, ins, outs, held, drain):
    l, y1, x2 = ins
    lp_s, y2_s = held
    lp_s[...] = -mm(l.get(), y1.get())
    drain.send(lp_s, outs[0])
    y2_s[...] = mm(x2.get(), lp_s[...])
    drain.send(y2_s, outs[1])


def next_body(core, ins, outs, held, drain):
    ln, y3, y2, x3, v3, z3, x2, vz2 = ins
    lnp_s, lnn_s, a_s, o_s = held
    out = outs[0]
    mine, _ = core_rows(core, HALF)
    lnp_s[...] = -mm(ln.get(), y3.get())
    lnn_s[...] = -mm(lnp_s[mine, :], y2.get())
    drain.send(lnn_s, out.at[pl.ds(HALF, HALF)])
    a_s[0:HALF, :] = mm(ln.ref()[mine, :], x3.get())
    a_s[HALF : HALF + ROWS, :] = v3.get()
    a_s[HALF + ROWS :, :] = z3.get()
    o_s[...] = mm(a_s[...], ln.get(), nt=True)
    a_s[0:HALF, :] = mm(lnp_s[mine, :], x2.get())
    a_s[HALF:, :] = vz2.get()
    o_s[...] = o_s[...] + mm(a_s[...], lnp_s[...], nt=True)
    drain.send(o_s.at[pl.ds(0, HALF)], out.at[pl.ds(0, HALF)])
    drain.send(o_s.at[pl.ds(HALF, HALF)], out.at[pl.ds(N, HALF)])


def left_body(core, ins, outs, held, drain):
    l1, y1, v1, z1, lp, y2, vz2, d, c, b = ins
    t_s, a_s, e_s = held
    mine, _ = core_rows(core, HALF)
    t_s[...] = l1.get().T
    e_s[0:HALF, :] = mm(t_s[mine, :], y1.get())
    a_s[0:ROWS, :] = v1.get()
    a_s[ROWS:, :] = z1.get()
    e_s[HALF:, :] = mm(a_s[...], l1.get())
    t_s[...] = lp.get().T
    e_s[0:HALF, :] = d.ref()[mine, :] - (e_s[0:HALF, :] + mm(t_s[mine, :], y2.get()))
    both = e_s[HALF:, :] + mm(vz2.get(), lp.get())
    e_s[HALF : HALF + ROWS, :] = c.get() - both[0:ROWS]
    e_s[HALF + ROWS :, :] = b.get() - both[ROWS:]
    drain.send(e_s, outs[0])


def place_body(core, ins, outs, held, drain):
    for feed, (out, which) in zip(ins, ((0, 1), (0, 3), (0, 2), (1, 1), (1, 3), (1, 2), (2, 1), (2, 3), (3, 1), (3, 3))):
        drain.send(feed.ref(), outs[out].at[which])
    vz2 = ins[10].ref()
    drain.send(vz2.at[pl.ds(0, ROWS)], outs[2].at[2])
    drain.send(vz2.at[pl.ds(ROWS, COLS)], outs[3].at[2])


def half_body(core, ins, outs, held, drain):
    e, n = ins
    h_s, r_s = held
    h_s[0:HALF, :] = e.ref()[0:HALF, :] - n.ref()[0:HALF, :]
    h_s[HALF:, :] = n.ref()[HALF : 2 * HALF, :]
    drain.send(h_s, outs[0])
    r_s[...] = e.ref()[HALF:, :] - n.ref()[N:, :]
    drain.send(r_s, outs[1])


def final_body(core, ins, outs, held, drain):
    top, right, s6, q6, q7, s8, q8 = ins
    sum_s, block_s, right_s = held
    a = s6.get() + q8.get()
    sum_s[...] = jnp.where(core == 0, s8.get() + q8.get(), a + (q6.get() + q7.get()))
    block_s[...] = top.get() - sum_s[0:ROWS]
    drain.send(block_s, outs[0])
    right_s[...] = right.get() - sum_s[ROWS:]
    drain.send(right_s, outs[1])


def kept_body(core, ins, outs, held, drain):
    h, hx, rest = ins
    mine, other = core_rows(core, HALF)
    for half, where in ((h, mine), (hx, other)):
        ref = half.ref()
        drain.send(ref.at[pl.ds(0, HALF)], outs[0].at[0, where])
        drain.send(ref.at[pl.ds(HALF, HALF)], outs[1].at[0, where])
    ref = rest.ref()
    drain.send(ref.at[pl.ds(0, ROWS)], outs[2].at[0])
    drain.send(ref.at[pl.ds(ROWS, COLS)], outs[3].at[0])


RINGS = {"y": (4, 32), "x": (4, 8), "z": (8, 1)}
ORDERS = (
    (("z", 0), ("z", 1), ("z", 0), ("z", 1), ("x", 0), ("x", 1), ("y", 0), ("y", 1)),
    (("x", 0), ("x", 1), ("y", 0), ("y", 1), ("z", 0), ("z", 1), ("z", 0), ("z", 1)),
)


def partner(index, ring, odd):
    size, stride = RINGS[ring]
    place = index // stride % size
    to = (place + (1 if place % 2 == odd else size - 1)) % size
    return index + (to - place) * stride


def step(value, number):
    route = []
    for index in range(lax.axis_size("tm")):
        for core in range(2):
            ring, odd = ORDERS[core][number]
            route.append((index * 2 + core, partner(index, ring, odd) * 2 + core))
    return lax.ppermute(value, ("tm", "rhs"), route)


def sum_over_tm(v, first):
    q1 = step(v, 0)
    a = v + q1
    q2 = step(a, 1)
    s3 = jnp.where(first, q2, a + q2)
    q3 = step(s3, 2)
    s4 = jnp.where(first, q3, s3 + q3)
    q4 = step(s4, 3)
    s5 = jnp.where(first, (a + q4) + (q2 + q3), s4 + q4)
    q5 = step(s5, 4)
    s6 = s5 + q5
    q6 = step(s6, 5)
    s7 = jnp.where(first, s6 + q6, q6)
    q7 = step(s7, 6)
    s8 = jnp.where(first, s7 + q7, q7)
    q8 = step(s8, 7)
    return s6, q6, q7, s8, q8


def swapped(value):
    return lax.ppermute(value, "rhs", [(0, 1), (1, 0)])


def along(value, distance, core=None):
    devices = range(lax.axis_size("tm"))
    pairs = [(i, i + distance) for i in devices if i + distance in devices]
    cores = (0, 1) if core is None else (core,)
    route = [(i * 2 + c, j * 2 + c) for i, j in pairs for c in cores]
    return lax.ppermute(value, ("tm", "rhs"), route)


def per_device(diag, link, arrow, right, arrow_block, arrow_rhs):
    core = lax.axis_index("rhs")
    first = core == 0
    me = jnp.reshape(core, (1,)).astype(jnp.int32)
    square = (N, N)
    right = jnp.swapaxes(right, 1, 2)
    arrow_x = swapped(arrow)
    right_x = swapped(right)

    strip = (ROWS, N)
    slim = (COLS, N)
    x, t, w, link_0 = call(
        inverse_body, me,
        [(square, [(diag, own)]), (square, [(link, lambda ref, c: ref.at[2 + c])]), (square, [(link, at(0))])],
        [square] * 4, scratch=[square] * 3, units=24,
    )
    t_x = swapped(t)
    link_n = along(link_0, -1)
    snd, keep = call(
        own_body, me,
        [
            (square, [(x, whole)]), (strip, [(arrow, own)]), (strip, [(arrow_x, own)]), (slim, [(right, own)]),
            (slim, [(right_x, own)]), (square, [(link, own)]), (square, [(w, whole)]),
        ],
        [(1472, N), (448, N)],
        scratch=[(256, N), (ROWS, N), square, square, square, square], units=4,
    )
    rcv = swapped(snd)
    (x2,) = call(
        inverse2_body, me,
        [(square, [(diag, at(2))]), (square, [(t, whole)]), (square, [(t_x, whole)])],
        [square], scratch=[square, square], units=22,
    )
    vz2, sums = call(
        arrow_body, me,
        [
            (square, [(x2, whole)]), (strip, [(arrow, at(2))]), (strip, [(arrow_x, at(2))]),
            ((256, N), [(snd, rows(768, 256))]), ((256, N), [(rcv, rows(768, 256))]), (slim, [(right, at(2))]),
            (slim, [(keep, rows(192, COLS))]), (slim, [(rcv, rows(1216, COLS))]),
            (strip, [(keep, rows(256, ROWS))]), (strip, [(rcv, rows(1280, ROWS))]),
            (slim, [(keep, rows(384, COLS))]), (slim, [(rcv, rows(1408, COLS))]),
        ],
        [(HALF, N), (HALF, 256)], scratch=[(256, N), (HALF, N), (HALF, 256)], units=2,
    )
    pieces = sum_over_tm(sums, first)

    x_1 = (square, [(snd, rows(0, N)), (rcv, rows(0, N))])
    x_3 = (square, [(rcv, rows(0, N)), (snd, rows(0, N))])
    y_1 = (square, [(snd, rows(N, N)), (rcv, rows(N, N))])
    y_3 = (square, [(rcv, rows(N, N)), (snd, rows(N, N))])
    v_1 = (strip, [(keep, rows(0, ROWS)), (rcv, rows(1024, ROWS))])
    v_3 = (strip, [(rcv, rows(1024, ROWS)), (keep, rows(0, ROWS))])
    z_1 = (slim, [(keep, rows(128, COLS)), (rcv, rows(1152, COLS))])
    z_3 = (slim, [(rcv, rows(1152, COLS)), (keep, rows(128, COLS))])
    x_2 = (square, [(x2, whole)])
    vz_2 = ((HALF, N), [(vz2, whole)])
    l_n = (square, [(link_n, whole)])
    link_p, y2 = call(
        link_body, me, [(square, [(link, at(2))]), y_1, x_2],
        [square, square], scratch=[square, square], room=ROOM, units=2,
    )
    l_p = (square, [(link_p, whole)])
    y_2 = (square, [(y2, whole)])
    (ahead,) = call(
        next_body, me, [l_n, y_3, y_2, x_3, v_3, z_3, x_2, vz_2],
        [(576, N)], scratch=[square, (HALF, N), square, square], room=ROOM, units=4.5,
    )
    behind1 = along(ahead, 1, 1)
    behind0 = along(ahead, 1, 0)
    (edge,) = call(
        left_body, me,
        [
            (square, [(link, at(1))]), y_1, v_1, z_1, l_p, y_2, vz_2,
            (square, [(diag, at(0))]), (strip, [(arrow, at(0))]), (slim, [(right, at(0))]),
        ],
        [square], scratch=[square, (HALF, N), square], room=ROOM, units=2,
    )
    placed = call(
        place_body, me, [x_1, x_3, x_2, y_1, y_3, y_2, v_1, v_3, z_1, z_3, vz_2],
        [(4, N, N), (4, N, N), (4, ROWS, N), (4, COLS, N)], room=ROOM, units=0.1,
    )
    halves, rest = call(
        half_body, me, [(square, [(edge, whole)]), ((576, N), [(behind0, whole), (behind1, whole)])],
        [square, (HALF, N)], scratch=[square, (HALF, N)], room=ROOM, units=0.1,
    )
    halves_x = swapped(halves)
    outs = call(
        kept_body, me,
        [(square, [(halves, whole)]), (square, [(halves_x, whole)]), ((HALF, N), [(rest, whole)])],
        [(4, N, N), (4, N, N), (4, ROWS, N), (4, COLS, N)], room=ROOM, units=0.1, alias=placed,
    )
    reduced, reduced_right = call(
        final_body, me,
        [((ROWS, 256), [(arrow_block, whole)]), ((COLS, 256), [(jnp.swapaxes(arrow_rhs, 0, 1), whole)])]
        + [((HALF, 256), [(piece, whole)]) for piece in pieces],
        [(ROWS, 256), (COLS, 256)], scratch=[(HALF, 256), (ROWS, 256), (COLS, 256)], room=ROOM, units=0.1,
    )
    return outs[0], outs[1], outs[2], jnp.swapaxes(outs[3], 1, 2), reduced, jnp.swapaxes(reduced_right, 0, 1)


def solution(mesh):
    placements = (P("tm", None, None), P("tm", None, None), P("tm", "rhs", None), P("tm", None, "rhs"),
                  P("rhs", None), P(None, "rhs"))
    return jax.shard_map(per_device, mesh=mesh, in_specs=placements, out_specs=placements, check_vma=False)
```

```python
import jax
import jax.numpy as jnp
from jax import lax
from jax.experimental import pallas as pl
from jax.experimental.pallas import tpu as pltpu
from jax.sharding import PartitionSpec as P


ITERS = 12
N = 384
HALF = 192
ROWS = 128
COLS = 64
F32 = jnp.float32
B16 = jnp.bfloat16
VMEM = 67043328
ROOM = 600 << 10


def dot(a, b, nt):
    dims = (((1,), (1 if nt else 0,)), ((), ()))
    return lax.dot_general(a, b, dims, preferred_element_type=F32)


def parts(x):
    high = x.astype(B16)
    return high, (x - high.astype(F32)).astype(B16)


def mm(a, b, nt=False):
    ah, al = parts(a)
    bh, bl = parts(b)
    n = b.shape[0] if nt else b.shape[1]
    if n % 128 == 0:
        both = dot(ah, jnp.concatenate([bh, bl], 0 if nt else 1), nt)
        return both[:, :n] + (both[:, n:] + dot(al, bh, nt))
    return dot(ah, bh, nt) + (dot(ah, bl, nt) + dot(al, bh, nt))


def newton(m_ref, x_ref):
    m = m_ref[...]
    row_bound = jnp.max(jnp.sum(jnp.abs(m), axis=1, keepdims=True), axis=0, keepdims=True)
    scale = 1.0 / row_bound
    eye = (
        lax.broadcasted_iota(jnp.int32, (N, N), 0) == lax.broadcasted_iota(jnp.int32, (N, N), 1)
    ).astype(F32)
    x_ref[...] = 2.0 * (eye * scale) - (m * scale) * scale

    def sweep(counter, carry):
        x = x_ref[...]
        residual = eye - mm(m_ref[...], x)
        x_ref[...] = x + mm(x, residual)
        return carry

    lax.fori_loop(0, ITERS - 1, sweep, 0)


class Feed:
    def __init__(self, core, sources, buf, sem):
        self.copy = pltpu.make_async_copy(sources[0], buf, sem)
        self.buf = buf
        self.ready = False
        if len(sources) == 1:
            self.copy.start()
        else:
            for which, source in enumerate(sources):

                @pl.when(core == which)
                def _(source=source):
                    pltpu.make_async_copy(source, buf, sem).start()

    def ref(self):
        if not self.ready:
            self.copy.wait()
            self.ready = True
        return self.buf

    def get(self):
        return self.ref()[...]


class Drain:
    def __init__(self, sems):
        self.sems = sems
        self.copies = []

    def send(self, src, dst):
        copy = pltpu.make_async_copy(src, dst, self.sems.at[len(self.copies)])
        copy.start()
        self.copies.append(copy)

    def finish(self):
        for copy in self.copies:
            copy.wait()


OUT_COPIES = 16


def call(body, me, ins, outs, scratch=(), units=1.0, alias=None, room=0):
    arrays = []
    places = []
    for shape, sources in ins:
        found = []
        for array, view in sources:
            for number, known in enumerate(arrays):
                if known is array:
                    break
            else:
                number = len(arrays)
                arrays.append(array)
            found.append((number, view))
        places.append(found)
    count = len(arrays)
    extra = list(alias or ())

    def kernel(core_ref, *refs):
        core = core_ref[0]
        given = refs[:count]
        outputs = refs[count + len(extra) : count + len(extra) + len(outs)]
        rest = refs[count + len(extra) + len(outs) :]
        bufs, held, in_sems, out_sems = rest[: len(ins)], rest[len(ins) : -2], rest[-2], rest[-1]
        feeds = [
            Feed(core, [view(given[number], core) for number, view in found], buf, in_sems.at[i])
            for i, (found, buf) in enumerate(zip(places, bufs))
        ]
        drain = Drain(out_sems)
        body(core, feeds, outputs, held, drain)
        drain.finish()

    moved = sum(4 * a.size for a in arrays)
    far = pl.BlockSpec(memory_space=pltpu.HBM)
    return pl.pallas_call(
        kernel,
        out_shape=[jax.ShapeDtypeStruct(shape, F32) for shape in outs],
        in_specs=[pl.BlockSpec(memory_space=pltpu.SMEM)] + [far] * (count + len(extra)),
        out_specs=[far] * len(outs),
        scratch_shapes=[pltpu.VMEM(shape, F32) for shape, sources in ins]
        + [pltpu.VMEM(shape, F32) for shape in scratch]
        + [pltpu.SemaphoreType.DMA((len(ins),)), pltpu.SemaphoreType.DMA((OUT_COPIES,))],
        input_output_aliases={1 + count + i: i for i in range(len(extra))},
        compiler_params=pltpu.CompilerParams(vmem_limit_bytes=VMEM - room),
        cost_estimate=pl.CostEstimate(flops=int(units * 6 * N**3), bytes_accessed=moved, transcendentals=0),
    )(me, *arrays, *extra)


def whole(ref, core):
    return ref


def rows(start, size):
    return lambda ref, core: ref.at[pl.ds(start, size)]


def at(index):
    return lambda ref, core: ref.at[index]


def own(ref, core):
    return ref.at[1 + 2 * core]


def core_rows(core, size):
    mine = pl.multiple_of(core * size, size)
    other = pl.multiple_of((1 - core) * size, size)
    return pl.ds(mine, size), pl.ds(other, size)


def inverse_body(core, ins, outs, held, drain):
    d, l, l0 = ins
    x_out, t_out, w_out, l0_out = outs
    x_s, t_s, w_s = held
    drain.send(l0.ref(), l0_out)
    newton(d.ref(), x_s)
    drain.send(x_s, x_out)
    l_ref = l.ref()

    @pl.when(core == 0)
    def _():
        w_s[...] = l_ref[...]

    @pl.when(core == 1)
    def _():
        w_s[...] = l_ref[...].T

    drain.send(w_s, w_out)
    w = w_s[...]
    t_s[...] = mm(mm(w, x_s[...]), w, nt=True)
    drain.send(t_s, t_out)


def own_body(core, ins, outs, held, drain):
    x_in, c_in, cx_in, b_in, bx_in, l_in, w_in = ins
    snd, keep = outs
    full, b_s, vz_s, gh_s, blk_s, y_s = held
    mine, other = core_rows(core, ROWS)
    full[mine, :] = c_in.get()
    full[other, :] = cx_in.get()
    b_s[0:COLS, :] = b_in.get()
    b_s[COLS:, :] = bx_in.get()
    x = x_in.get()
    drain.send(x_in.ref(), snd.at[pl.ds(0, N)])
    c = full[...]
    vz_s[0:256, :] = mm(c, x)
    vz_s[256:384, :] = mm(b_s[...], x, nt=True)
    drain.send(vz_s.at[other], snd.at[pl.ds(1024, ROWS)])
    drain.send(vz_s.at[pl.ds(320, COLS)], snd.at[pl.ds(1152, COLS)])
    drain.send(vz_s.at[mine], keep.at[pl.ds(0, ROWS)])
    drain.send(vz_s.at[pl.ds(256, COLS)], keep.at[pl.ds(128, COLS)])
    y_s[...] = mm(x, l_in.get())
    drain.send(y_s, snd.at[pl.ds(N, N)])
    vz = vz_s[...]
    gh_s[...] = mm(vz, w_in.get(), nt=True)
    drain.send(gh_s.at[pl.ds(0, 256)], snd.at[pl.ds(768, 256)])
    drain.send(gh_s.at[pl.ds(320, COLS)], snd.at[pl.ds(1216, COLS)])
    drain.send(gh_s.at[pl.ds(256, COLS)], keep.at[pl.ds(192, COLS)])
    blk_s[:, 0:256] = mm(vz, c, nt=True)
    drain.send(blk_s.at[other], snd.at[pl.ds(1280, ROWS)])
    drain.send(blk_s.at[pl.ds(320, COLS)], snd.at[pl.ds(1408, COLS)])
    drain.send(blk_s.at[mine], keep.at[pl.ds(256, ROWS)])
    drain.send(blk_s.at[pl.ds(256, COLS)], keep.at[pl.ds(384, COLS)])


def inverse2_body(core, ins, outs, held, drain):
    d, t, tx = ins
    m_s, x_s = held
    m_s[...] = d.get() - (t.get() + tx.get())
    newton(m_s, x_s)
    drain.send(x_s, outs[0])


def arrow_body(core, ins, outs, held, drain):
    x_in, c_in, cx_in, g, gx, b_in, hk, hr, bk, br, rk, rr = ins
    full, vz_s, s_s = held
    mine, other = core_rows(core, ROWS)
    full[mine, :] = c_in.get()
    full[other, :] = cx_in.get()
    full[...] = full[...] - (g.get() + gx.get())
    b = b_in.get() - (hk.get() + hr.get())
    x = x_in.get()
    vz_s[0:ROWS, :] = mm(full[mine, :], x)
    vz_s[ROWS:, :] = mm(b, x, nt=True)
    drain.send(vz_s, outs[0])
    sums = mm(vz_s[...], full[...], nt=True)
    s_s[0:ROWS, :] = sums[0:ROWS] + (bk.ref()[:, 0:256] + br.ref()[:, 0:256])
    s_s[ROWS:, :] = sums[ROWS:] + (rk.ref()[:, 0:256] + rr.ref()[:, 0:256])
    drain.send(s_s, outs[1])


def link_body(core, ins, outs, held, drain):
    l, y1, x2 = ins
    lp_s, y2_s = held
    lp_s[...] = -mm(l.get(), y1.get())
    drain.send(lp_s, outs[0])
    y2_s[...] = mm(x2.get(), lp_s[...])
    drain.send(y2_s, outs[1])


def next_body(core, ins, outs, held, drain):
    ln, y3, y2, x3, v3, z3, x2, vz2 = ins
    lnp_s, lnn_s, a_s, o_s = held
    out_d, out_l, out_c = outs
    mine, _ = core_rows(core, HALF)
    lnp_s[...] = -mm(ln.get(), y3.get())
    lnn_s[...] = -mm(lnp_s[mine, :], y2.get())
    drain.send(lnn_s, out_l)
    a_s[0:HALF, :] = mm(ln.ref()[mine, :], x3.get())
    a_s[HALF : HALF + ROWS, :] = v3.get()
    a_s[HALF + ROWS :, :] = z3.get()
    o_s[...] = mm(a_s[...], ln.get(), nt=True)
    a_s[0:HALF, :] = mm(lnp_s[mine, :], x2.get())
    a_s[HALF:, :] = vz2.get()
    o_s[...] = o_s[...] + mm(a_s[...], lnp_s[...], nt=True)
    drain.send(o_s.at[pl.ds(0, HALF)], out_d)
    drain.send(o_s.at[pl.ds(HALF, HALF)], out_c)


def left_body(core, ins, outs, held, drain):
    l1, y1, v1, z1, lp, y2, vz2, d, c, b = ins
    a_s, e_s = held
    e_s[0:N, :] = mm(l1.get().T, y1.get())
    a_s[0:ROWS, :] = v1.get()
    a_s[ROWS:, :] = z1.get()
    e_s[N:, :] = mm(a_s[...], l1.get())
    e_s[0:N, :] = d.get() - (e_s[0:N, :] + mm(lp.get().T, y2.get()))
    drain.send(e_s.at[pl.ds(0, N)], outs[0].at[pl.ds(0, N)])
    both = e_s[N:, :] + mm(vz2.get(), lp.get())
    e_s[N : N + ROWS, :] = c.get() - both[0:ROWS]
    e_s[N + ROWS :, :] = b.get() - both[ROWS:]
    drain.send(e_s.at[pl.ds(N, HALF)], outs[0].at[pl.ds(N, HALF)])


def place_body(core, ins, outs, held, drain):
    for feed, (out, which) in zip(ins, ((0, 1), (0, 3), (0, 2), (1, 1), (1, 3), (1, 2), (2, 1), (2, 3), (3, 1), (3, 3))):
        drain.send(feed.ref(), outs[out].at[which])
    vz2 = ins[10].ref()
    drain.send(vz2.at[pl.ds(0, ROWS)], outs[2].at[2])
    drain.send(vz2.at[pl.ds(ROWS, COLS)], outs[3].at[2])


def final_body(core, ins, outs, held, drain):
    top, right, value, other = ins
    block_s, right_s = held
    total = value.get() + other.get()
    block_s[...] = top.get() - total[0:ROWS]
    drain.send(block_s, outs[0])
    right_s[...] = right.get() - total[ROWS:]
    drain.send(right_s, outs[1])


def kept_body(core, ins, outs, held, drain):
    edge, near_d, far_d, near_l, far_l, near_c = ins
    d_s, c_s = held
    mine, other = core_rows(core, HALF)
    e = edge.ref()
    drain.send(near_l.ref(), outs[1].at[0, mine])
    drain.send(far_l.ref(), outs[1].at[0, other])
    d_s[mine, :] = e[mine, :] - near_d.get()
    d_s[other, :] = e[other, :] - far_d.get()
    drain.send(d_s, outs[0].at[0])
    c_s[...] = e[N:, :] - near_c.get()
    drain.send(c_s.at[pl.ds(0, ROWS)], outs[2].at[0])
    drain.send(c_s.at[pl.ds(ROWS, COLS)], outs[3].at[0])


RINGS = {"y": (4, 32), "x": (4, 8), "z": (8, 1)}
ORDERS = (
    (("z", 0), ("z", 1), ("z", 0), ("z", 1), ("x", 0), ("x", 1), ("y", 0), ("y", 1)),
    (("z", 0), ("z", 1), ("z", 0), ("z", 1), ("y", 0), ("y", 1), ("x", 0), ("x", 1)),
)


def partner(index, ring, odd):
    size, stride = RINGS[ring]
    place = index // stride % size
    to = (place + (1 if place % 2 == odd else size - 1)) % size
    return index + (to - place) * stride


def step(value, number):
    route = []
    for index in range(lax.axis_size("tm")):
        for core in range(2):
            ring, odd = ORDERS[core][number]
            route.append((index * 2 + core, partner(index, ring, odd) * 2 + core))
    return lax.ppermute(value, ("tm", "rhs"), route)


def sum_over_tm(v):
    a = v + step(v, 0)
    near = step(a, 1)
    far = step(near, 2)
    last = step(far, 3)
    value = (a + last) + (near + far)
    for number in range(4, 7):
        value = value + step(value, number)
    return value, step(value, 7)


def swapped(value):
    return lax.ppermute(value, "rhs", [(0, 1), (1, 0)])


def along(value, distance):
    devices = range(lax.axis_size("tm"))
    route = [(i, i + distance) for i in devices if i + distance in devices]
    return lax.ppermute(value, "tm", route)


def per_device(diag, link, arrow, right, arrow_block, arrow_rhs):
    core = lax.axis_index("rhs")
    me = jnp.reshape(core, (1,)).astype(jnp.int32)
    square = (N, N)
    right = jnp.swapaxes(right, 1, 2)
    arrow_x = swapped(arrow)
    right_x = swapped(right)

    strip = (ROWS, N)
    slim = (COLS, N)
    x, t, w, link_0 = call(
        inverse_body, me,
        [(square, [(diag, own)]), (square, [(link, lambda ref, c: ref.at[2 + c])]), (square, [(link, at(0))])],
        [square] * 4, scratch=[square] * 3, units=24,
    )
    t_x = swapped(t)
    link_n = along(link_0, -1)
    snd, keep = call(
        own_body, me,
        [
            (square, [(x, whole)]), (strip, [(arrow, own)]), (strip, [(arrow_x, own)]), (slim, [(right, own)]),
            (slim, [(right_x, own)]), (square, [(link, own)]), (square, [(w, whole)]),
        ],
        [(1472, N), (448, N)],
        scratch=[(256, N), (ROWS, N), square, square, square, square], units=4,
    )
    rcv = swapped(snd)
    (x2,) = call(
        inverse2_body, me,
        [(square, [(diag, at(2))]), (square, [(t, whole)]), (square, [(t_x, whole)])],
        [square], scratch=[square, square], units=22,
    )
    vz2, sums = call(
        arrow_body, me,
        [
            (square, [(x2, whole)]), (strip, [(arrow, at(2))]), (strip, [(arrow_x, at(2))]),
            ((256, N), [(snd, rows(768, 256))]), ((256, N), [(rcv, rows(768, 256))]), (slim, [(right, at(2))]),
            (slim, [(keep, rows(192, COLS))]), (slim, [(rcv, rows(1216, COLS))]),
            (strip, [(keep, rows(256, ROWS))]), (strip, [(rcv, rows(1280, ROWS))]),
            (slim, [(keep, rows(384, COLS))]), (slim, [(rcv, rows(1408, COLS))]),
        ],
        [(HALF, N), (HALF, 256)], scratch=[(256, N), (HALF, N), (HALF, 256)], units=2,
    )
    pieces = sum_over_tm(sums)

    x_1 = (square, [(snd, rows(0, N)), (rcv, rows(0, N))])
    x_3 = (square, [(rcv, rows(0, N)), (snd, rows(0, N))])
    y_1 = (square, [(snd, rows(N, N)), (rcv, rows(N, N))])
    y_3 = (square, [(rcv, rows(N, N)), (snd, rows(N, N))])
    v_1 = (strip, [(keep, rows(0, ROWS)), (rcv, rows(1024, ROWS))])
    v_3 = (strip, [(rcv, rows(1024, ROWS)), (keep, rows(0, ROWS))])
    z_1 = (slim, [(keep, rows(128, COLS)), (rcv, rows(1152, COLS))])
    z_3 = (slim, [(rcv, rows(1152, COLS)), (keep, rows(128, COLS))])
    x_2 = (square, [(x2, whole)])
    vz_2 = ((HALF, N), [(vz2, whole)])
    l_n = (square, [(link_n, whole)])
    link_p, y2 = call(
        link_body, me, [(square, [(link, at(2))]), y_1, x_2],
        [square, square], scratch=[square, square], room=ROOM, units=2,
    )
    l_p = (square, [(link_p, whole)])
    y_2 = (square, [(y2, whole)])
    ahead_d, ahead_l, ahead_c = call(
        next_body, me, [l_n, y_3, y_2, x_3, v_3, z_3, x_2, vz_2],
        [(HALF, N)] * 3, scratch=[square, (HALF, N), square, square], room=ROOM, units=4.5,
    )
    behind_d = along(ahead_d, 1)
    behind_l = along(ahead_l, 1)
    behind_c = along(ahead_c, 1)
    far_d = swapped(behind_d)
    far_l = swapped(behind_l)
    (edge,) = call(
        left_body, me,
        [
            (square, [(link, at(1))]), y_1, v_1, z_1, l_p, y_2, vz_2,
            (square, [(diag, at(0))]), (strip, [(arrow, at(0))]), (slim, [(right, at(0))]),
        ],
        [(576, N)], scratch=[(HALF, N), (576, N)], room=ROOM, units=3,
    )
    placed = call(
        place_body, me, [x_1, x_3, x_2, y_1, y_3, y_2, v_1, v_3, z_1, z_3, vz_2],
        [(4, N, N), (4, N, N), (4, ROWS, N), (4, COLS, N)], room=ROOM, units=0.1,
    )
    outs = call(
        kept_body, me,
        [((576, N), [(edge, whole)])]
        + [((HALF, N), [(part, whole)]) for part in (behind_d, far_d, behind_l, far_l, behind_c)],
        [(4, N, N), (4, N, N), (4, ROWS, N), (4, COLS, N)], scratch=[square, (HALF, N)], room=ROOM, units=0.1,
        alias=placed,
    )
    reduced, reduced_right = call(
        final_body, me,
        [((ROWS, 256), [(arrow_block, whole)]), ((COLS, 256), [(jnp.swapaxes(arrow_rhs, 0, 1), whole)])]
        + [((HALF, 256), [(piece, whole)]) for piece in pieces],
        [(ROWS, 256), (COLS, 256)], scratch=[(ROWS, 256), (COLS, 256)], room=ROOM, units=0.1,
    )
    return outs[0], outs[1], outs[2], jnp.swapaxes(outs[3], 1, 2), reduced, jnp.swapaxes(reduced_right, 0, 1)


def solution(mesh):
    placements = (P("tm", None, None), P("tm", None, None), P("tm", "rhs", None), P("tm", None, "rhs"),
                  P("rhs", None), P(None, "rhs"))
    return jax.shard_map(per_device, mesh=mesh, in_specs=placements, out_specs=placements, check_vma=False)
```
